32 devices in a mesh: dp: 32 (over z, y, x, core).
Axes of the slice: x: 2, y: 2, z: 4, core: 2. Of those that a mesh axis runs over, the one named last changes fastest.
Arguments:
- tokens: bfloat16 [4096, 1088], P('dp'), may hold values from -6 to 6
- seq_lengths: int32 [8], replicated, may hold values from 1 to 1024, as said below
- w_qkv: bfloat16 [3551232], P('dp'), may hold values from -8 to 8
- w_out: bfloat16 [1183744], P('dp'), may hold values from -0.75 to 0.75
- w_up: bfloat16 [4734976], P('dp'), may hold values from -0.1875 to 0.1875
- w_down: bfloat16 [4734976], P('dp'), may hold values from -0.09375 to 0.09375
- vectors: bfloat16 [16384], P('dp'), may hold values from -4 to 4
- cotangent: bfloat16 [4096, 1088], P('dp'), may hold values from -6 to 6
Outputs:
- out_block: bfloat16 [4096, 1088], P('dp')
- grad_tokens: float32 [4096, 1088], P('dp')
- grad_w_qkv: float32 [3551232], P('dp')
- grad_w_out: float32 [1183744], P('dp')
- grad_w_up: float32 [4734976], P('dp')
- grad_w_down: float32 [4734976], P('dp')
- grad_vectors: float32 [16384], P('dp')
The draws below stay inside these ranges and needn't reach their ends.
Inputs may be any that keep to these rules, and one draw needn't show every extreme that they name: `seq_lengths`: sequences are packed end to end, each padded to whole blocks of 128 tokens, and together they fill exactly 32 blocks; a sequence covers at most 8 blocks, and some sequence covers exactly 8 full blocks.
All inputs are finite; a program needn't handle non-finite values.
Results may differ from the reference program's by a relative error of at most 0.0084.
Values may be sent and summed in bfloat16 or wider, within the bound.
A program may use at most 256 MiB of HBM per device.

```python
import jax
import jax.numpy as jnp
from jax import lax

D = 1088
HEADS = 17
HEAD = 64
FF = 4352
BLOCK = 128
MAXB = 8
NBLK = 32
NSEQ = 8
QKV_LEN = 3551232
OUT_LEN = 1183744
FF_LEN = 4734976
VEC_LEN = 16384


def draw_seq_lengths(key, part):
    key_pairs = jax.random.fold_in(key, 11)
    key_order = jax.random.fold_in(key, 12)
    key_tail = jax.random.fold_in(key, 13)
    pair_count = (NSEQ - 4) // 2
    shifted = jax.random.randint(key_pairs, (pair_count,), -3, 4, dtype=jnp.int32)
    fixed_part = jnp.array([MAXB, 2, 2, 4], dtype=jnp.int32)
    counts = jnp.concatenate([fixed_part, 4 + shifted, 4 - shifted]).astype(jnp.int32)
    order = jax.random.permutation(key_order, NSEQ)
    counts = counts[order]
    tails = jax.random.randint(key_tail, (NSEQ,), 1, BLOCK + 1, dtype=jnp.int32)
    tails = jnp.where(counts == MAXB, BLOCK, tails)
    return ((counts - 1) * BLOCK + tails).astype(jnp.int32)


def draw_w_qkv(key, part):
    base = jax.random.normal(jax.random.fold_in(key, 21), (D, 3 * D), jnp.float32) * D ** (-0.5)
    spare = jax.random.normal(jax.random.fold_in(key, 23), (QKV_LEN - 3 * D * D,), jnp.float32) * D ** (-0.5)
    return jnp.clip(jnp.concatenate([base.reshape(-1), spare]), -8.0, 8.0).astype(jnp.bfloat16)


def draw_vectors(key, part):
    table = jnp.clip(jax.random.normal(jax.random.fold_in(key, 31), (12, D), jnp.float32) * 0.4, -2.0, 2.0)
    gains = 1.0 + 0.3 * jax.random.uniform(jax.random.fold_in(key, 32), (2, D), jnp.float32, -1.0, 1.0)
    table = table.at[0].set(gains[0]).at[5].set(gains[1])
    spare = jax.random.uniform(jax.random.fold_in(key, 33), (VEC_LEN - 12 * D,), jnp.float32, -1.0, 1.0)
    return jnp.concatenate([table.reshape(-1), spare]).astype(jnp.bfloat16)


def steps_of(key, dims, split, least, high):
    gain, own = 1.0, jax.random.fold_in(key, 6)
    for axis_at, shards_of in split:
        heights = jnp.exp(jax.random.uniform(jax.random.fold_in(own, axis_at), (shards_of,), jnp.float32, least / len(split), high / len(split)))
        gain = gain * jnp.repeat(heights, dims[axis_at] // shards_of).reshape([-1 if axis == axis_at else 1 for axis in range(len(dims))])
    return gain


def gaussian(own_key, extent, spread, bound, shards=(), kind=jnp.bfloat16):
    loudness = steps_of(own_key, extent, shards, -0.22, 0.18) if shards else 1.0
    values = jax.random.normal(own_key, extent, jnp.float32) * spread * loudness
    return jnp.minimum(jnp.maximum(values, -bound), bound).astype(kind)


def setup_inputs(seed: int = 0) -> dict:
    key_list = jax.random.split(jax.random.key(seed), 9)
    return {
        "tokens": gaussian(key_list[0], (NBLK * BLOCK, D), 1.0, 6.0, ((0, 32),)),
        "seq_lengths": draw_seq_lengths(jax.random.fold_in(key_list[8], 71), 0),
        "w_qkv": draw_w_qkv(jax.random.fold_in(key_list[8], 71), 0),
        "w_out": gaussian(key_list[3], (OUT_LEN,), (D // 16) ** -0.5, 0.75, ((0, 32),)),
        "w_up": gaussian(key_list[4], (FF_LEN,), D ** -0.5, 0.1875, ((0, 32),)),
        "w_down": gaussian(key_list[5], (FF_LEN,), FF ** -0.5, 0.09375, ((0, 32),)),
        "vectors": draw_vectors(jax.random.fold_in(key_list[8], 71), 0),
        "cotangent": gaussian(key_list[7], (NBLK * BLOCK, D), 1.0, 6.0, ((0, 32),)),
    }


EPS = 1e-05

def block_layout(seq_lengths, block_ids):
    counts = ((seq_lengths + BLOCK - 1) // BLOCK).astype(jnp.int32)
    end_pos = jnp.cumsum(counts).astype(jnp.int32)
    start_pos = (end_pos - counts).astype(jnp.int32)
    owns_block = (block_ids[:, None] >= start_pos[None, :]) & (block_ids[:, None] < end_pos[None, :])
    first_blk = lax.optimization_barrier(jnp.sum(jnp.where(owns_block, start_pos[None, :], 0), axis=1)).astype(jnp.int32)
    seq_len = lax.optimization_barrier(jnp.sum(jnp.where(owns_block, seq_lengths[None, :], 0), axis=1)).astype(jnp.int32)
    inside = (block_ids - first_blk).astype(jnp.int32)
    filled = jnp.clip(seq_len - inside * BLOCK, 0, BLOCK).astype(jnp.int32)
    return (inside, filled)

def window_mask(inside):
    row_ids = jnp.arange(BLOCK, dtype=jnp.int32)[:, None]
    col_ids = jnp.arange(MAXB * BLOCK, dtype=jnp.int32)[None, :]
    slot_ids = col_ids // BLOCK
    return (slot_ids <= inside) & ((slot_ids > 0) | (col_ids <= row_ids))

def layer_norm(values, gain_vec, bias_vec):
    average = lax.optimization_barrier(jnp.mean(values, axis=-1, keepdims=True))
    centred = values - average
    variance = lax.optimization_barrier(jnp.mean(centred * centred, axis=-1, keepdims=True))
    inv_std = lax.rsqrt(variance + EPS)
    normalized = centred * inv_std
    return (normalized * gain_vec + bias_vec, normalized, inv_std)

def norm_back(grad_out, normalized, inv_std, gain_vec):
    grad_hat = grad_out * gain_vec
    first_mean = lax.optimization_barrier(jnp.mean(grad_hat, axis=-1, keepdims=True))
    second_mean = lax.optimization_barrier(jnp.mean(grad_hat * normalized, axis=-1, keepdims=True))
    return inv_std * (grad_hat - first_mean - normalized * second_mean)

def split_heads(matrix):
    return matrix.reshape(matrix.shape[0], HEADS, HEAD).transpose(1, 0, 2)

def join_heads(matrix):
    return matrix.transpose(1, 0, 2).reshape(matrix.shape[1], HEADS * HEAD)

def head_forward(query, keys, values, allowed):
    scores = jnp.dot(query, keys.T, preferred_element_type=jnp.float32)
    scores = jnp.where(allowed, scores, -1e+30)
    row_max = lax.optimization_barrier(jnp.max(scores, axis=-1))
    row_total = lax.optimization_barrier(jnp.sum(jnp.exp(scores - row_max[:, None]), axis=-1))
    log_sums = row_max + jnp.log(row_total)
    prob_bf = jnp.where(allowed, jnp.exp(scores - log_sums[:, None]), 0.0).astype(jnp.bfloat16)
    output = jnp.dot(prob_bf, values, preferred_element_type=jnp.float32).astype(jnp.bfloat16)
    return (output, log_sums)

def head_backward(query, keys, values, output, grad_output, log_sums, allowed):
    scores = jnp.dot(query, keys.T, preferred_element_type=jnp.float32)
    probs = jnp.where(allowed, jnp.exp(scores - log_sums[:, None]), 0.0)
    prob_bf = probs.astype(jnp.bfloat16)
    grad_value = jnp.dot(prob_bf.T, grad_output, preferred_element_type=jnp.float32)
    grad_prob = jnp.dot(grad_output, values.T, preferred_element_type=jnp.float32)
    row_delta = lax.optimization_barrier(jnp.sum(grad_output.astype(jnp.float32) * output.astype(jnp.float32), axis=-1))
    grad_score = (probs * (grad_prob - row_delta[:, None])).astype(jnp.bfloat16)
    grad_query = jnp.dot(grad_score, keys, preferred_element_type=jnp.float32)
    grad_key = jnp.dot(grad_score.T, query, preferred_element_type=jnp.float32)
    return (grad_query, grad_key, grad_value)

def attend(query, keys, values, allowed):

    def one_head(packed):
        return head_forward(packed[0], packed[1], packed[2], allowed)
    outputs, log_sums = lax.map(one_head, (split_heads(query), split_heads(keys), split_heads(values)))
    return (join_heads(outputs), log_sums)

def attend_back(query, keys, values, output, grad_output, log_sums, allowed):

    def one_head(packed):
        return head_backward(packed[0], packed[1], packed[2], packed[3], packed[4], packed[5], allowed)
    grad_query, grad_key, grad_value = lax.map(one_head, (split_heads(query), split_heads(keys), split_heads(values), split_heads(output), split_heads(grad_output), log_sums))
    return (join_heads(grad_query), join_heads(grad_key), join_heads(grad_value))

def pad_flat(matrix, length):
    flat = matrix.reshape(-1)
    return jnp.concatenate([flat, jnp.zeros((length - flat.shape[0],), jnp.float32)])

def reference(tokens, seq_lengths, w_qkv, w_out, w_up, w_down, vectors, cotangent):
    total_rows = NBLK * BLOCK
    block_ids = jnp.arange(NBLK, dtype=jnp.int32)
    inside, filled = block_layout(seq_lengths, block_ids)
    valid = (jnp.arange(BLOCK, dtype=jnp.int32)[None, :] < filled[:, None]).reshape(total_rows)
    weight_qkv = w_qkv[:3 * D * D].reshape(D, 3 * D)
    weight_out = w_out[:D * D].reshape(D, D)
    weight_up = w_up[:D * FF].reshape(D, FF)
    weight_down = w_down[:FF * D].reshape(FF, D)
    vector_rows = vectors[:12 * D].reshape(12, D).astype(jnp.float32)
    bias_up = vector_rows[8:12].reshape(FF)
    query_scale = HEAD ** (-0.5)
    inputs = tokens.astype(jnp.float32)
    normed_attn, hat_one, inv_one = layer_norm(inputs, vector_rows[0], vector_rows[1])
    normed_attn = normed_attn.astype(jnp.bfloat16)
    projected = jnp.dot(normed_attn, weight_qkv, preferred_element_type=jnp.float32)
    query = (query_scale * (projected[:, :D] + vector_rows[2])).astype(jnp.bfloat16)
    keys = projected[:, D:2 * D].astype(jnp.bfloat16)
    values = (projected[:, 2 * D:] + vector_rows[3]).astype(jnp.bfloat16)
    kv_blocks = jnp.stack([keys.reshape(NBLK, BLOCK, D), values.reshape(NBLK, BLOCK, D)], axis=1)
    query_blocks = query.reshape(NBLK, BLOCK, D)

    def window(block_num):
        source_blk = block_num - jnp.arange(MAXB, dtype=jnp.int32)
        clipped = jnp.maximum(source_blk, 0)
        window_kv = kv_blocks[clipped]
        return (window_kv[:, 0].reshape(MAXB * BLOCK, D), window_kv[:, 1].reshape(MAXB * BLOCK, D))

    def forward_block(packed):
        block_num, query_blk, inside_blk = packed
        window_k, window_v = window(block_num)
        return attend(query_blk, window_k, window_v, window_mask(inside_blk))
    attended, log_sums = lax.map(forward_block, (block_ids, query_blocks, inside))
    attended = attended.reshape(total_rows, D)
    residual = inputs + jnp.dot(attended, weight_out, preferred_element_type=jnp.float32) + vector_rows[4]
    normed_mlp, hat_two, inv_two = layer_norm(residual, vector_rows[5], vector_rows[6])
    normed_mlp = normed_mlp.astype(jnp.bfloat16)
    up_pre = jnp.dot(normed_mlp, weight_up, preferred_element_type=jnp.float32) + bias_up
    normal_cdf = 0.5 * (1.0 + lax.erf(up_pre * 2.0 ** (-0.5)))
    activated = (up_pre * normal_cdf).astype(jnp.bfloat16)
    result = residual + jnp.dot(activated, weight_down, preferred_element_type=jnp.float32) + vector_rows[7]
    out_block = jnp.where(valid[:, None], result, 0.0).astype(jnp.bfloat16)
    cot_rows = jnp.where(valid[:, None], cotangent.astype(jnp.float32), 0.0)
    cot_bf = cot_rows.astype(jnp.bfloat16)
    grad_down = jnp.dot(activated.T, cot_bf, preferred_element_type=jnp.float32)
    grad_bias_down = lax.optimization_barrier(jnp.sum(cot_rows, axis=0))
    grad_act = jnp.dot(cot_bf, weight_down.T, preferred_element_type=jnp.float32)
    normal_pdf = jnp.exp(-0.5 * up_pre * up_pre) * (2.0 * jnp.pi) ** (-0.5)
    grad_pre = grad_act * (normal_cdf + up_pre * normal_pdf)
    grad_pre_bf = grad_pre.astype(jnp.bfloat16)
    grad_up = jnp.dot(normed_mlp.T, grad_pre_bf, preferred_element_type=jnp.float32)
    grad_bias_up = lax.optimization_barrier(jnp.sum(grad_pre, axis=0))
    grad_normed_mlp = jnp.dot(grad_pre_bf, weight_up.T, preferred_element_type=jnp.float32)
    grad_gain_two = lax.optimization_barrier(jnp.sum(grad_normed_mlp * hat_two, axis=0))
    grad_bias_two = lax.optimization_barrier(jnp.sum(grad_normed_mlp, axis=0))
    grad_residual = cot_rows + norm_back(grad_normed_mlp, hat_two, inv_two, vector_rows[5])
    grad_bias_out = lax.optimization_barrier(jnp.sum(grad_residual, axis=0))
    grad_res_bf = grad_residual.astype(jnp.bfloat16)
    grad_out = jnp.dot(attended.T, grad_res_bf, preferred_element_type=jnp.float32)
    grad_attended = jnp.dot(grad_res_bf, weight_out.T, preferred_element_type=jnp.float32).astype(jnp.bfloat16)

    def backward_block(dkv_total, packed):
        block_num, query_blk, attended_blk, grad_blk, sums_blk, inside_blk = packed
        window_k, window_v = window(block_num)
        grad_query, grad_key, grad_value = attend_back(query_blk, window_k, window_v, attended_blk, grad_blk, sums_blk, window_mask(inside_blk))
        window_grads = jnp.stack([grad_key.reshape(MAXB, BLOCK, D), grad_value.reshape(MAXB, BLOCK, D)], axis=1)
        in_window = jnp.arange(MAXB, dtype=jnp.int32) <= inside_blk
        window_grads = jnp.where(in_window[:, None, None, None], window_grads, 0.0)
        source_blk = jnp.maximum(block_num - jnp.arange(MAXB, dtype=jnp.int32), 0)
        return (dkv_total.at[source_blk].add(window_grads), grad_query)
    dkv_start = jnp.zeros((NBLK, 2, BLOCK, D), jnp.float32)
    dkv_total, grad_query = lax.scan(backward_block, dkv_start, (block_ids, query_blocks, attended.reshape(NBLK, BLOCK, D), grad_attended.reshape(NBLK, BLOCK, D), log_sums, inside))
    grad_query = query_scale * grad_query.reshape(total_rows, D)
    grad_key = dkv_total[:, 0].reshape(total_rows, D)
    grad_value = dkv_total[:, 1].reshape(total_rows, D)
    grad_project = jnp.concatenate([grad_query, grad_key, grad_value], axis=1).astype(jnp.bfloat16)
    grad_bias_q = lax.optimization_barrier(jnp.sum(grad_query, axis=0))
    grad_bias_v = lax.optimization_barrier(jnp.sum(grad_value, axis=0))
    grad_qkv = jnp.dot(normed_attn.T, grad_project, preferred_element_type=jnp.float32)
    grad_normed_attn = jnp.dot(grad_project, weight_qkv.T, preferred_element_type=jnp.float32)
    grad_gain_one = lax.optimization_barrier(jnp.sum(grad_normed_attn * hat_one, axis=0))
    grad_bias_one = lax.optimization_barrier(jnp.sum(grad_normed_attn, axis=0))
    grad_tokens = grad_residual + norm_back(grad_normed_attn, hat_one, inv_one, vector_rows[0])
    grad_vectors = jnp.concatenate([jnp.stack([grad_gain_one, grad_bias_one, grad_bias_q, grad_bias_v, grad_bias_out, grad_gain_two, grad_bias_two, grad_bias_down]), grad_bias_up.reshape(4, D)], axis=0)
    return (out_block, grad_tokens, pad_flat(grad_qkv, QKV_LEN), pad_flat(grad_out, OUT_LEN), pad_flat(grad_up, FF_LEN), pad_flat(grad_down, FF_LEN), pad_flat(grad_vectors, VEC_LEN))
```

```python
import jax
import jax.numpy as jnp
from jax import lax
from jax.experimental.layout import Layout, with_layout_constraint
from jax.sharding import PartitionSpec as P

D = 1088
HEADS = 17
HEAD = 64
FF = 4352
BLOCK = 128
MAXB = 8


EPS = 1e-05
WIRE = jnp.bfloat16


def shifted(value, axis, steps):
    count = lax.axis_size(axis)
    first, last = (max(0, -steps), min(count, count - steps))
    return lax.ppermute(value, axis, [(source, source + steps) for source in range(first, last)])


def block_layout(seq_lengths, block_ids):
    counts = (seq_lengths + BLOCK - 1) // BLOCK
    end_pos = jnp.cumsum(counts)
    start_pos = end_pos - counts
    owns_block = (block_ids[:, None] >= start_pos[None, :]) & (
        block_ids[:, None] < end_pos[None, :]
    )
    first_blk = jnp.sum(jnp.where(owns_block, start_pos[None, :], 0), axis=1)
    seq_len = jnp.sum(jnp.where(owns_block, seq_lengths[None, :], 0), axis=1)
    inside = block_ids - first_blk
    filled = jnp.clip(seq_len - inside * BLOCK, 0, BLOCK)
    return (inside, filled)


def window_mask(inside):
    row_ids = jnp.arange(BLOCK, dtype=jnp.int32)[:, None]
    col_ids = jnp.arange(MAXB * BLOCK, dtype=jnp.int32)[None, :]
    slot_ids = col_ids // BLOCK
    return (slot_ids <= inside) & ((slot_ids > 0) | (col_ids <= row_ids))


def layer_norm(values, gain_vec, bias_vec):
    average = jnp.mean(values, axis=-1, keepdims=True)
    centred = values - average
    variance = jnp.mean(centred * centred, axis=-1, keepdims=True)
    inv_std = lax.rsqrt(variance + EPS)
    normalized = centred * inv_std
    return (normalized * gain_vec + bias_vec, normalized, inv_std)


def norm_back(grad_out, normalized, inv_std, gain_vec):
    grad_hat = grad_out * gain_vec
    first_mean = jnp.mean(grad_hat, axis=-1, keepdims=True)
    second_mean = jnp.mean(grad_hat * normalized, axis=-1, keepdims=True)
    return inv_std * (grad_hat - first_mean - normalized * second_mean)


def split_heads(matrix):
    return matrix.reshape(matrix.shape[0], HEADS, HEAD).transpose(1, 0, 2)


def join_heads(matrix):
    return matrix.transpose(1, 0, 2).reshape(matrix.shape[1], HEADS * HEAD)


def head_forward(query, keys, values, allowed):
    scores = jnp.dot(query, keys.T, preferred_element_type=jnp.float32)
    scores = jnp.where(allowed, scores, -1e30)
    row_max = jnp.max(scores, axis=-1)
    row_total = jnp.sum(jnp.exp(scores - row_max[:, None]), axis=-1)
    log_sums = row_max + jnp.log(row_total)
    prob_bf = jnp.where(allowed, jnp.exp(scores - log_sums[:, None]), 0.0).astype(jnp.bfloat16)
    output = jnp.dot(prob_bf, values, preferred_element_type=jnp.float32).astype(jnp.bfloat16)
    return (output, log_sums)


def head_backward(query, keys, values, output, grad_output, log_sums, allowed):
    scores = jnp.dot(query, keys.T, preferred_element_type=jnp.float32)
    probs = jnp.where(allowed, jnp.exp(scores - log_sums[:, None]), 0.0)
    prob_bf = probs.astype(jnp.bfloat16)
    grad_value = jnp.dot(prob_bf.T, grad_output, preferred_element_type=jnp.float32)
    grad_prob = jnp.dot(grad_output, values.T, preferred_element_type=jnp.float32)
    row_delta = jnp.sum(grad_output.astype(jnp.float32) * output.astype(jnp.float32), axis=-1)
    grad_score = (probs * (grad_prob - row_delta[:, None])).astype(jnp.bfloat16)
    grad_query = jnp.dot(grad_score, keys, preferred_element_type=jnp.float32)
    grad_key = jnp.dot(grad_score.T, query, preferred_element_type=jnp.float32)
    return (grad_query, grad_key, grad_value)


def attend(query, keys, values, allowed):
    outputs, log_sums = jax.vmap(head_forward, (0, 0, 0, None))(
        split_heads(query), split_heads(keys), split_heads(values), allowed
    )
    return (join_heads(outputs), log_sums)


def attend_back(query, keys, values, output, grad_output, log_sums, allowed):
    grad_query, grad_key, grad_value = jax.vmap(head_backward, (0, 0, 0, 0, 0, 0, None))(
        split_heads(query),
        split_heads(keys),
        split_heads(values),
        split_heads(output),
        split_heads(grad_output),
        log_sums,
        allowed,
    )
    return (join_heads(grad_query), join_heads(grad_key), join_heads(grad_value))


def whole_rows(shard, rows, cols):
    count = lax.axis_size("dp")
    return shard.shape[0] % cols == 0 and shard.shape[0] * count == rows * cols


def gather_matrix(shard, rows, cols):
    if whole_rows(shard, rows, cols):
        return lax.all_gather(shard.reshape(-1, cols), "dp", axis=0, tiled=True)
    flat = lax.all_gather(shard, "dp", axis=0, tiled=True)
    return flat[: rows * cols].reshape(rows, cols)


def scatter_matrix(grad, shard):
    rows, cols = grad.shape
    grad = with_layout_constraint(grad.astype(WIRE), Layout((0, 1)))
    if whole_rows(shard, rows, cols):
        split = grad.reshape(lax.axis_size("dp"), -1, cols)
        own = lax.psum_scatter(split, "dp", scatter_dimension=0, tiled=False)
        return own.reshape(-1).astype(jnp.float32)
    flat = pad_flat(grad, shard.shape[0] * lax.axis_size("dp"))
    return lax.psum_scatter(flat, "dp", scatter_dimension=0, tiled=True).astype(jnp.float32)


def pad_flat(matrix, length):
    flat = matrix.reshape(-1)
    return jnp.concatenate([flat, jnp.zeros((length - flat.shape[0],), flat.dtype)])


def local(tokens, seq_lengths, w_qkv, w_out, w_up, w_down, vectors, cotangent):
    device_pos = lax.axis_index("dp")
    inside_all, filled_all = block_layout(seq_lengths, jnp.reshape(device_pos, (1,)))
    inside = inside_all[0]
    valid = jnp.arange(BLOCK, dtype=jnp.int32) < filled_all[0]
    allowed = window_mask(inside)
    vec_length = vectors.shape[0] * lax.axis_size("dp")
    vector_rows = lax.all_gather(vectors, "dp", axis=0, tiled=True)
    vector_rows = vector_rows[: 12 * D].reshape(12, D).astype(jnp.float32)
    weight_qkv = gather_matrix(w_qkv, D, 3 * D)
    weight_out = gather_matrix(w_out, D, D)
    weight_up = gather_matrix(w_up, D, FF)
    weight_down = gather_matrix(w_down, FF, D)
    bias_up = vector_rows[8:12].reshape(FF)
    query_scale = HEAD ** (-0.5)
    inputs = tokens.astype(jnp.float32)
    normed_attn, hat_one, inv_one = layer_norm(inputs, vector_rows[0], vector_rows[1])
    normed_attn = normed_attn.astype(jnp.bfloat16)
    projected = jnp.dot(normed_attn, weight_qkv, preferred_element_type=jnp.float32)
    query = (query_scale * (projected[:, :D] + vector_rows[2])).astype(jnp.bfloat16)
    keys = projected[:, D : 2 * D].astype(jnp.bfloat16)
    values = (projected[:, 2 * D :] + vector_rows[3]).astype(jnp.bfloat16)
    key_value = jnp.stack([keys, values])
    pieces = [key_value]
    for offset in range(1, MAXB):
        pieces.append(shifted(key_value, "dp", offset))
    window_kv = jnp.stack(pieces)
    window_k = window_kv[:, 0].reshape(MAXB * BLOCK, D)
    window_v = window_kv[:, 1].reshape(MAXB * BLOCK, D)
    attended, log_sums = attend(query, window_k, window_v, allowed)
    residual = (
        inputs + jnp.dot(attended, weight_out, preferred_element_type=jnp.float32) + vector_rows[4]
    )
    normed_mlp, hat_two, inv_two = layer_norm(residual, vector_rows[5], vector_rows[6])
    normed_mlp = normed_mlp.astype(jnp.bfloat16)
    up_pre = jnp.dot(normed_mlp, weight_up, preferred_element_type=jnp.float32) + bias_up
    normal_cdf = 0.5 * (1.0 + lax.erf(up_pre * 2.0 ** (-0.5)))
    activated = (up_pre * normal_cdf).astype(jnp.bfloat16)
    result = (
        residual
        + jnp.dot(activated, weight_down, preferred_element_type=jnp.float32)
        + vector_rows[7]
    )
    out_block = jnp.where(valid[:, None], result, 0.0).astype(jnp.bfloat16)
    cot_rows = jnp.where(valid[:, None], cotangent.astype(jnp.float32), 0.0)
    cot_bf = cot_rows.astype(jnp.bfloat16)
    grad_down = jnp.dot(activated.T, cot_bf, preferred_element_type=jnp.float32)
    grad_bias_down = jnp.sum(cot_rows, axis=0)
    grad_act = jnp.dot(cot_bf, weight_down.T, preferred_element_type=jnp.float32)
    normal_pdf = jnp.exp(-0.5 * up_pre * up_pre) * (2.0 * jnp.pi) ** (-0.5)
    grad_pre = grad_act * (normal_cdf + up_pre * normal_pdf)
    grad_pre_bf = grad_pre.astype(jnp.bfloat16)
    grad_up = jnp.dot(normed_mlp.T, grad_pre_bf, preferred_element_type=jnp.float32)
    grad_bias_up = jnp.sum(grad_pre, axis=0)
    grad_normed_mlp = jnp.dot(grad_pre_bf, weight_up.T, preferred_element_type=jnp.float32)
    grad_gain_two = jnp.sum(grad_normed_mlp * hat_two, axis=0)
    grad_bias_two = jnp.sum(grad_normed_mlp, axis=0)
    grad_residual = cot_rows + norm_back(grad_normed_mlp, hat_two, inv_two, vector_rows[5])
    grad_bias_out = jnp.sum(grad_residual, axis=0)
    grad_res_bf = grad_residual.astype(jnp.bfloat16)
    grad_out = jnp.dot(attended.T, grad_res_bf, preferred_element_type=jnp.float32)
    grad_attended = jnp.dot(grad_res_bf, weight_out.T, preferred_element_type=jnp.float32).astype(
        jnp.bfloat16
    )
    grad_down, grad_up, grad_out, grad_attended = lax.optimization_barrier(
        (grad_down.astype(WIRE), grad_up.astype(WIRE), grad_out.astype(WIRE), grad_attended)
    )
    shard_down = scatter_matrix(grad_down, w_down)
    shard_up = scatter_matrix(grad_up, w_up)
    shard_out = scatter_matrix(grad_out, w_out)
    grad_query, grad_key, grad_value = attend_back(
        query, window_k, window_v, attended, grad_attended, log_sums, allowed
    )
    grad_query, grad_key, grad_value, shard_down = lax.optimization_barrier(
        (grad_query, grad_key, grad_value, shard_down)
    )
    window_grads = jnp.stack(
        [grad_key.reshape(MAXB, BLOCK, D), grad_value.reshape(MAXB, BLOCK, D)], axis=1
    )
    sent_grads = window_grads.astype(WIRE)
    own_grads = window_grads[0]
    for offset in range(1, MAXB):
        own_grads = own_grads + shifted(sent_grads[offset], "dp", -offset).astype(jnp.float32)
    grad_query = query_scale * grad_query
    grad_project = jnp.concatenate([grad_query, own_grads[0], own_grads[1]], axis=1).astype(
        jnp.bfloat16
    )
    grad_project, shard_up, shard_out = lax.optimization_barrier(
        (grad_project, shard_up, shard_out)
    )
    grad_bias_q = jnp.sum(grad_query, axis=0)
    grad_bias_v = jnp.sum(own_grads[1], axis=0)
    grad_qkv = jnp.dot(normed_attn.T, grad_project, preferred_element_type=jnp.float32)
    grad_normed_attn = jnp.dot(grad_project, weight_qkv.T, preferred_element_type=jnp.float32)
    grad_gain_one = jnp.sum(grad_normed_attn * hat_one, axis=0)
    grad_bias_one = jnp.sum(grad_normed_attn, axis=0)
    grad_tokens = grad_residual + norm_back(grad_normed_attn, hat_one, inv_one, vector_rows[0])
    grad_vectors = jnp.concatenate(
        [
            jnp.stack(
                [
                    grad_gain_one,
                    grad_bias_one,
                    grad_bias_q,
                    grad_bias_v,
                    grad_bias_out,
                    grad_gain_two,
                    grad_bias_two,
                    grad_bias_down,
                ]
            ),
            grad_bias_up.reshape(4, D),
        ],
        axis=0,
    )
    shard_qkv = scatter_matrix(grad_qkv, w_qkv)
    shard_vec = lax.psum_scatter(
        pad_flat(grad_vectors, vec_length), "dp", scatter_dimension=0, tiled=True
    )
    return (out_block, grad_tokens, shard_qkv, shard_out, shard_up, shard_down, shard_vec)


def solution(mesh):
    in_specs = (P("dp", None), P(), P("dp"), P("dp"), P("dp"), P("dp"), P("dp"), P("dp", None))
    out_specs = (P("dp", None), P("dp", None), P("dp"), P("dp"), P("dp"), P("dp"), P("dp"))
    return jax.shard_map(local, mesh=mesh, in_specs=in_specs, out_specs=out_specs, check_vma=False)
```
